32 devices in a mesh: rows: 8 (over z, y), cols: 4 (over x, core).
Axes of the slice: x: 2, y: 2, z: 4, core: 2. Of those that a mesh axis runs over, the one named last changes fastest.
Arguments:
- hamiltonian: bfloat16 [16384, 1728], P('rows'), may hold values from -0.15625 to 0.15625
- neighbors: int32 [256, 27], P('rows'), may hold values from 0 to 255, as said below
- neighbor_counts: int32 [256], P('rows'), may hold values from 9 to 27, as said below
- interval: float32 [2], replicated, may hold values from -1 to 1, as said below
- vectors: bfloat16 [16384, 1024], P('rows', 'cols'), may hold values from -6 to 6
Outputs:
- projected_ham: float32 [1024, 1024], P('rows', 'cols')
- intersection: float32 [1024, 1024], P('rows', 'cols')
The draws below stay inside these ranges and needn't reach their ends.
Inputs may be any that keep to these rules, and one draw needn't show every extreme that they name: neighbors[b, 0] = b; every entry lies within 32 blocks of b, cyclically over 256 blocks. `neighbor_counts`: block 0 uses all slots. interval[0] < 0 < interval[1].
All inputs are finite; a program needn't handle non-finite values.
Results may differ from the reference program's by a relative error of at most 0.0065.
Values may be sent and summed in bfloat16 or wider, within the bound.
No kernel may reach another device: no remote copies, remote signals or barrier semaphores. Data moves between devices by JAX's collectives and lax.ppermute only.
A program may use at most 128 MiB of HBM per device.

```python
import jax
import jax.numpy as jnp
from jax import lax

ORB = 64
NBR = 27
VEC = 1024
DEG = 4
BLK_DEV = 32
NB = 256
NROWS = 16384


def draw_neighbors(key, part):
    offsets = jax.random.randint(jax.random.fold_in(key, 11), (NB, NBR), -BLK_DEV, BLK_DEV + 1)
    offsets = offsets.at[:, 0].set(0)
    return ((jnp.arange(NB, dtype=jnp.int32)[:, None] + offsets) % NB).astype(jnp.int32)


def draw_neighbor_counts(key, part):
    counts = jax.random.randint(jax.random.fold_in(key, 23), (NB,), NBR // 3, NBR + 1)
    return counts.at[0].set(NBR).astype(jnp.int32)


def draw_interval(key, part):
    values = jax.random.uniform(jax.random.fold_in(key, 37), (2,), jnp.float32)
    lower = -0.6 - 0.4 * values[0]
    upper = 0.6 + 0.4 * values[1]
    return jnp.stack([lower, upper]).astype(jnp.float32)


def strengthened(drawn, own_key, source, target, blocks, factor):
    def block_of(axis_at):
        return (jnp.arange(drawn.shape[axis_at]) // (drawn.shape[axis_at] // blocks)).reshape((-1,) + (1,) * (drawn.ndim - 1 - axis_at))

    first = jax.random.permutation(own_key, blocks)[block_of(target)]
    other_side = (block_of(target) + blocks // 2) % blocks
    return jnp.where((block_of(source) == first) | (block_of(source) == other_side), factor * drawn, drawn)


def shard_levels(own_key, dims, pieces, smallest, high):
    factor_of = 1.0
    for dim, shards_of in pieces:
        draws = jax.random.uniform(jax.random.fold_in(jax.random.fold_in(own_key, 6), dim), (shards_of,), jnp.float32, smallest / len(pieces), high / len(pieces))
        factor_of = factor_of * jnp.repeat(jnp.exp(draws), dims[dim] // shards_of).reshape((-1,) + (1,) * (len(dims) - 1 - dim))
    return factor_of


def gaussian(rng, shape, spread, bound, pieces=(), held_as=jnp.bfloat16):
    entries = spread * jax.random.normal(rng, shape, jnp.float32)
    if pieces:
        entries = entries * shard_levels(rng, shape, pieces, -0.22, 0.18)
    return jnp.clip(entries, -bound, bound).astype(held_as)


def bell_draw_with(own_key, shape, width, most, shards, heavy, kind=jnp.bfloat16):
    values = width * jax.random.normal(own_key, shape, jnp.float32)
    if shards:
        values = values * shard_levels(own_key, shape, shards, -0.22, 0.18)
    return jnp.clip(strengthened(values, jax.random.fold_in(own_key, 3), *heavy), -most, most).astype(kind)


def setup_inputs(seed: int = 0) -> dict:
    key_list = jax.random.split(jax.random.key(seed), 6)
    return {
        "hamiltonian": gaussian(key_list[0], (NROWS, NBR * ORB), (NBR * ORB) ** -0.5, 0.15625, ((0, 8),)),
        "neighbors": draw_neighbors(jax.random.fold_in(key_list[5], 71), 0),
        "neighbor_counts": draw_neighbor_counts(jax.random.fold_in(key_list[5], 71), 0),
        "interval": draw_interval(jax.random.fold_in(key_list[5], 71), 0),
        "vectors": bell_draw_with(key_list[4], (NROWS, VEC), 1.0, 6.0, ((0, 8), (1, 4)), (0, 1, 8, 2.0)),
    }


def apply_ham(masked, neighbors, field):
    blocked = field.reshape(NB, ORB, VEC)
    ham_groups = masked.reshape(NB // BLK_DEV, BLK_DEV, ORB, NBR * ORB)
    nbr_groups = neighbors.reshape(NB // BLK_DEV, BLK_DEV, NBR)

    def one_group(pair):
        ham_part, nbr_part = pair
        gathered = blocked[nbr_part].reshape(BLK_DEV, NBR * ORB, VEC)
        return jnp.einsum("bik,bkc->bic", ham_part.astype(jnp.float32), gathered.astype(jnp.float32))

    result = lax.map(one_group, (ham_groups, nbr_groups))
    return result.reshape(NROWS, VEC)


def reference(hamiltonian, neighbors, neighbor_counts, interval, vectors):
    used = jnp.arange(NBR)[None, :] < neighbor_counts[:, None]
    used_cols = jnp.repeat(used, ORB, axis=1)
    used_rows = jnp.repeat(used_cols, ORB, axis=0)
    masked = jnp.where(used_rows, hamiltonian, jnp.zeros_like(hamiltonian))
    center = (interval[0] + interval[1]) / 2.0
    half_width = (interval[1] - interval[0]) / 2.0
    previous = vectors
    current = ((apply_ham(masked, neighbors, previous) - center * previous.astype(jnp.float32)) / half_width).astype(jnp.bfloat16)
    for iteration in range(DEG - 1):
        product = apply_ham(masked, neighbors, current)
        following = (2.0 * (product - center * current.astype(jnp.float32)) / half_width - previous.astype(jnp.float32)).astype(jnp.bfloat16)
        previous, current = current, following
    image = apply_ham(masked, neighbors, current).astype(jnp.bfloat16)
    projected_ham = jnp.dot(current.T, image, preferred_element_type=jnp.float32) / NROWS
    intersection = jnp.dot(current.T, current, preferred_element_type=jnp.float32) / NROWS
    return projected_ham, intersection
```

```python
import functools

import jax
import jax.numpy as jnp
from jax import lax
from jax.experimental import pallas as pl
from jax.experimental.pallas import tpu as pltpu
from jax.sharding import PartitionSpec as P

DEG = 4
LANES = 128
GROUP = 4
STEP = 4
PIECES = 2


def mask_body(counts, ham_t, out, *, orbitals):
    step = pl.program_id(0)
    depth, lanes = ham_t.shape
    row = lax.broadcasted_iota(jnp.int32, (lanes, lanes), 0)
    col = lax.broadcasted_iota(jnp.int32, (lanes, lanes), 1)
    per = lanes // orbitals
    limit = jnp.zeros((lanes, lanes), jnp.int32)
    for i in range(per):
        limit = jnp.where(row // orbitals == i, counts[step * per + i] * orbitals, limit)
    for start in range(0, out.shape[1], lanes):
        size = min(lanes, depth - start)
        if size <= 0:
            out[:, start : start + lanes] = jnp.zeros((lanes, lanes), out.dtype)
            continue
        tile = ham_t[start : start + size, :].astype(jnp.float32)
        if size < lanes:
            tile = jnp.concatenate([tile, jnp.zeros((lanes - size, lanes), jnp.float32)], axis=0)
        tile = jnp.where(col + start < limit, tile.T, 0.0)
        out[:, start : start + lanes] = tile.astype(out.dtype)


def masked_rows(hamiltonian, counts, orbitals):
    rows, depth = hamiltonian.shape
    padded = pl.cdiv(depth, GROUP * orbitals) * GROUP * orbitals
    return pl.pallas_call(
        functools.partial(mask_body, orbitals=orbitals),
        out_shape=jax.ShapeDtypeStruct((rows, padded), hamiltonian.dtype),
        grid_spec=pltpu.PrefetchScalarGridSpec(
            num_scalar_prefetch=1,
            grid=(rows // LANES,),
            in_specs=[pl.BlockSpec((depth, LANES), lambda g, c: (0, g))],
            out_specs=pl.BlockSpec((LANES, padded), lambda g, c: (g, 0)),
        ),
        compiler_params=pltpu.CompilerParams(vmem_limit_bytes=16 << 20),
        cost_estimate=pl.CostEstimate(
            flops=rows * padded, bytes_accessed=4 * rows * padded, transcendentals=0
        ),
        name="masked_rows",
    )(counts, hamiltonian.T)


def apply_body(index, interval, *refs, kind, pieces, orbitals):
    ham = refs[0]
    sources = refs[1 : 1 + 3 * pieces]
    at = 1 + 3 * pieces
    older = refs[at : at + pieces] if kind == "next" else ()
    at += len(older)
    outs = refs[at : at + pieces]
    extended = refs[at + pieces]
    step = pl.program_id(0)
    length = sources[0].shape[0]
    tile = GROUP * orbitals
    groups = ham.shape[1] // tile

    @pl.when(step == 0)
    def _():
        for i, source in enumerate(sources):
            extended[i * length : (i + 1) * length, :] = source[...]

    center = (interval[0] + interval[1]) / 2.0
    half_width = (interval[1] - interval[0]) / 2.0
    for j in range(STEP):
        block = step * STEP + j
        total = None
        for group in range(groups):
            parts = []
            for slot in range(group * GROUP, (group + 1) * GROUP):
                start = pl.multiple_of(index[block * groups * GROUP + slot] * orbitals, orbitals)
                parts.append(extended[pl.ds(start, orbitals), :])
            term = jnp.dot(
                ham[j * orbitals : (j + 1) * orbitals, group * tile : (group + 1) * tile],
                jnp.concatenate(parts, axis=0),
                preferred_element_type=jnp.float32,
            )
            total = term if total is None else total + term
        if kind != "image":
            own = extended[pl.ds(pl.multiple_of(block * orbitals, orbitals), orbitals), :]
            total = total - center * own.astype(jnp.float32)
            total = total / half_width if kind == "first" else 2.0 * total / half_width
        steps = length // (STEP * orbitals)
        for i in range(pieces):

            @pl.when(step // steps == i)
            def _():
                rows = pl.ds(pl.multiple_of(block * orbitals - i * length, orbitals), orbitals)
                value = total
                if kind == "next":
                    value = value - older[i][rows, :].astype(jnp.float32)
                outs[i][rows, :] = value.astype(outs[i].dtype)


def apply_ham(masked, index, interval, kind, own, near, far, older, orbitals):
    pieces = len(own)
    length, width = own[0].shape
    slab = length * pieces
    padded = masked.shape[1]
    arrays = [*own, *near, *far, *(older if kind == "next" else ())]
    whole = pl.BlockSpec((length, width), lambda g, *_: (0, 0))
    return pl.pallas_call(
        functools.partial(apply_body, kind=kind, pieces=pieces, orbitals=orbitals),
        out_shape=[jax.ShapeDtypeStruct((length, width), own[0].dtype)] * pieces,
        grid_spec=pltpu.PrefetchScalarGridSpec(
            num_scalar_prefetch=2,
            grid=(slab // (STEP * orbitals),),
            in_specs=[pl.BlockSpec((STEP * orbitals, padded), lambda g, *_: (g, 0))]
            + [whole] * len(arrays),
            out_specs=[whole] * pieces,
            scratch_shapes=[pltpu.VMEM((3 * slab, width), own[0].dtype)],
        ),
        compiler_params=pltpu.CompilerParams(vmem_limit_bytes=16 << 20),
        cost_estimate=pl.CostEstimate(
            flops=2 * slab * padded * width,
            bytes_accessed=2 * slab * padded + 2 * slab * width * 5,
            transcendentals=0,
        ),
        name="apply_" + kind,
    )(index, interval, masked, *arrays)


def exchange(own):
    count = lax.axis_size("rows")
    swap = [(i, i ^ 1) for i in range(count)]
    onward = [(i, (i + 2) % count if i % 2 == 0 else (i - 2) % count) for i in range(count)]
    near = [lax.ppermute(piece, "rows", swap) for piece in own]
    far = [lax.ppermute(piece, "rows", onward) for piece in near]
    return near, far


def shards(hamiltonian, neighbors, neighbor_counts, interval, vectors):
    blocks, slots = neighbors.shape
    slab_rows = hamiltonian.shape[0]
    orbitals = slab_rows // blocks
    count = lax.axis_size("rows")
    order = slab_rows * count
    width = vectors.shape[1]
    streams = width // LANES
    length = slab_rows // PIECES
    masked = masked_rows(hamiltonian, neighbor_counts, orbitals)

    me = lax.axis_index("rows")
    slab = neighbors // blocks
    place = jnp.where(slab == me, 0, jnp.where(slab == (me ^ 1), 1, 2))
    index = place * blocks + neighbors % blocks
    padded = masked.shape[1] // orbitals
    index = jnp.concatenate(
        [index, jnp.broadcast_to(index[:, :1], (blocks, padded - slots))], axis=1
    ).reshape(-1)

    def run(kind, own, halo, older=None):
        return apply_ham(masked, index, interval, kind, own, *halo, older, orbitals)

    current = [
        [
            vectors[i * length : (i + 1) * length, s * LANES : (s + 1) * LANES]
            for i in range(PIECES)
        ]
        for s in range(streams)
    ]
    older = [None] * streams
    for step in range(DEG):
        for s in range(streams):
            kind = "first" if step == 0 else "next"
            new = run(kind, current[s], exchange(current[s]), older[s])
            older[s], current[s] = current[s], new
    images = [run("image", own, exchange(own)) for own in current]

    joined = jnp.concatenate(
        [jnp.concatenate([a[i] for a in images + current], axis=1) for i in range(PIECES)], axis=0
    )
    contract = (((0,), (0,)), ((), ()))
    terms = []
    for s in range(streams):
        every = lax.all_gather(jnp.concatenate(current[s], axis=0), "cols", axis=1, tiled=True)
        term = lax.dot_general(every, joined, contract, preferred_element_type=jnp.float32)
        terms.append(term.reshape(-1, 1, LANES, 2 * width))
    terms = jnp.concatenate(terms, axis=1).reshape(-1, 2 * width)
    summed = lax.psum_scatter(terms, "rows", scatter_dimension=0, tiled=True)
    return summed[:, :width] / order, summed[:, width:] / order


def solution(mesh):
    in_specs = (P("rows", None), P("rows", None), P("rows"), P(), P("rows", "cols"))
    out_specs = (P("rows", "cols"), P("rows", "cols"))
    return jax.shard_map(shards, mesh=mesh, in_specs=in_specs, out_specs=out_specs, check_vma=False)
```

```python
import functools

import jax
import jax.numpy as jnp
from jax import lax
from jax.experimental import pallas as pl
from jax.experimental.pallas import tpu as pltpu
from jax.sharding import PartitionSpec as P

DEG = 4
LANES = 128
GROUP = 4
STEP = 16
PIECES = 2
WIRE = jnp.float32


def mask_body(counts, ham_t, out, *, orbitals):
    step = pl.program_id(0)
    depth, lanes = ham_t.shape
    row = lax.broadcasted_iota(jnp.int32, (lanes, lanes), 0)
    col = lax.broadcasted_iota(jnp.int32, (lanes, lanes), 1)
    per = lanes // orbitals
    limit = jnp.zeros((lanes, lanes), jnp.int32)
    for i in range(per):
        limit = jnp.where(row // orbitals == i, counts[step * per + i] * orbitals, limit)
    for start in range(0, out.shape[1], lanes):
        size = min(lanes, depth - start)
        if size <= 0:
            out[:, start : start + lanes] = jnp.zeros((lanes, lanes), out.dtype)
            continue
        tile = ham_t[start : start + size, :].astype(jnp.float32)
        if size < lanes:
            tile = jnp.concatenate([tile, jnp.zeros((lanes - size, lanes), jnp.float32)], axis=0)
        tile = jnp.where(col + start < limit, tile.T, 0.0)
        out[:, start : start + lanes] = tile.astype(out.dtype)


def masked_rows(hamiltonian, counts, orbitals):
    rows, depth = hamiltonian.shape
    padded = pl.cdiv(depth, GROUP * orbitals) * GROUP * orbitals
    return pl.pallas_call(
        functools.partial(mask_body, orbitals=orbitals),
        out_shape=jax.ShapeDtypeStruct((rows, padded), hamiltonian.dtype),
        grid_spec=pltpu.PrefetchScalarGridSpec(
            num_scalar_prefetch=1,
            grid=(rows // LANES,),
            in_specs=[pl.BlockSpec((depth, LANES), lambda g, c: (0, g))],
            out_specs=pl.BlockSpec((LANES, padded), lambda g, c: (g, 0)),
        ),
        compiler_params=pltpu.CompilerParams(vmem_limit_bytes=16 << 20),
        cost_estimate=pl.CostEstimate(
            flops=rows * padded, bytes_accessed=4 * rows * padded, transcendentals=0
        ),
        name="masked_rows",
    )(counts, hamiltonian.T)


def apply_body(index, interval, *refs, kind, pieces, part, orbitals):
    ham = refs[0]
    sources = refs[1 : 1 + 3 * pieces]
    older = refs[1 + 3 * pieces] if kind == "next" else None
    out, extended = refs[-2:]
    length = sources[0].shape[0]
    tile = GROUP * orbitals
    groups = ham.shape[1] // tile
    for i, source in enumerate(sources):
        extended[i * length : (i + 1) * length, :] = source[...]
    center = (interval[0] + interval[1]) / 2.0
    half_width = (interval[1] - interval[0]) / 2.0

    def run(step, carry):
        for j in range(STEP):
            block = step * STEP + j
            rows = pl.ds(pl.multiple_of(block * orbitals, orbitals), orbitals)
            whole_rows = pl.ds(
                pl.multiple_of(part * length + block * orbitals, orbitals), orbitals
            )
            first = (part * length // orbitals + block) * groups * GROUP
            total = None
            for group in range(groups):
                parts = []
                for slot in range(group * GROUP, (group + 1) * GROUP):
                    start = pl.multiple_of(index[first + slot] * orbitals, orbitals)
                    parts.append(extended[pl.ds(start, orbitals), :])
                term = jnp.dot(
                    ham[whole_rows, group * tile : (group + 1) * tile],
                    jnp.concatenate(parts, axis=0),
                    preferred_element_type=jnp.float32,
                )
                total = term if total is None else total + term
            if kind != "image":
                total = total - center * extended[whole_rows, :].astype(jnp.float32)
                total = total / half_width if kind == "first" else 2.0 * total / half_width
            if kind == "next":
                total = total - older[rows, :].astype(jnp.float32)
            out[rows, :] = total.astype(out.dtype)
        return carry

    lax.fori_loop(0, length // (STEP * orbitals), run, 0)


def apply_ham(masked, index, interval, kind, part, own, near, far, older, orbitals):
    pieces = len(own)
    length, width = own[0].shape
    slab = length * pieces
    padded = masked.shape[1]
    arrays = [*own, *near, *far, *([older[part]] if kind == "next" else [])]
    in_vmem = pl.BlockSpec(memory_space=pltpu.VMEM)
    return pl.pallas_call(
        functools.partial(apply_body, kind=kind, pieces=pieces, part=part, orbitals=orbitals),
        out_shape=jax.ShapeDtypeStruct((length, width), own[0].dtype),
        grid_spec=pltpu.PrefetchScalarGridSpec(
            num_scalar_prefetch=2,
            grid=(),
            in_specs=[in_vmem] * (1 + len(arrays)),
            out_specs=in_vmem,
            scratch_shapes=[pltpu.VMEM((3 * slab, width), own[0].dtype)],
        ),
        compiler_params=pltpu.CompilerParams(vmem_limit_bytes=20 << 20),
        cost_estimate=pl.CostEstimate(
            flops=2 * length * padded * width,
            bytes_accessed=2 * length * padded + 2 * slab * width * 4,
            transcendentals=0,
        ),
        name="apply_" + kind,
    )(index, interval, masked, *arrays)


def after(value, *done):
    return lax.optimization_barrier((value, *done))[0]


def pair_of(i):
    return i ^ 1


def swap(piece):
    count = lax.axis_size("rows")
    return lax.ppermute(piece, "rows", [(i, pair_of(i)) for i in range(count)])


def onward(piece):
    count = lax.axis_size("rows")
    pairs = [(i, (i + 2) % count if i % 2 == 0 else (i - 2) % count) for i in range(count)]
    return lax.ppermute(piece, "rows", pairs)


def scattered(terms):
    count = lax.axis_size("rows")
    pairs = count // 2
    me = lax.axis_index("rows")
    mine = lax.dynamic_index_in_dim(terms, me % 2, 2, keepdims=False)
    other = lax.dynamic_index_in_dim(terms, 1 - me % 2, 2, keepdims=False)
    both = mine + swap(other.astype(WIRE)).astype(jnp.float32)
    here = me // 2
    total = lax.dynamic_index_in_dim(both, here, 1, keepdims=False)
    for shift in range(1, pairs):
        away = lax.dynamic_index_in_dim(both, (here + shift) % pairs, 1, keepdims=False)
        hops = [(i, (i + 2 * shift) % count) for i in range(count)]
        total = total + lax.ppermute(away.astype(WIRE), "rows", hops).astype(jnp.float32)
    return total


def shards(hamiltonian, neighbors, neighbor_counts, interval, vectors):
    blocks, slots = neighbors.shape
    slab_rows = hamiltonian.shape[0]
    orbitals = slab_rows // blocks
    count = lax.axis_size("rows")
    order = slab_rows * count
    width = vectors.shape[1]
    streams = width // LANES
    length = slab_rows // PIECES
    masked = masked_rows(hamiltonian, neighbor_counts, orbitals)

    me = lax.axis_index("rows")
    slab = neighbors // blocks
    place = jnp.where(slab == me, 0, jnp.where(slab == pair_of(me), 1, 2))
    index = place * blocks + neighbors % blocks
    padded = masked.shape[1] // orbitals
    index = jnp.concatenate(
        [index, jnp.broadcast_to(index[:, :1], (blocks, padded - slots))], axis=1
    ).reshape(-1)

    own = [
        [
            vectors[i * length : (i + 1) * length, s * LANES : (s + 1) * LANES]
            for i in range(PIECES)
        ]
        for s in range(streams)
    ]
    older = [None] * streams
    near = [[swap(piece) for piece in own[s]] for s in range(streams)]
    last = None
    every = [None] * streams
    for step in range(DEG + 1):
        kind = "first" if step == 0 else "next" if step < DEG else "image"
        for s in range(streams):
            far = [onward(piece) for piece in near[s]]
            new, coming = [], []
            for part in range(PIECES):
                done = [] if last is None else [last]
                if streams > 1 and (step > 0 or s > 0) and near[s - 1]:
                    done.append(near[s - 1][part])
                last = apply_ham(
                    masked, after(index, *done), interval, kind, part, own[s], near[s], far,
                    older[s], orbitals,
                )
                new.append(last)
                if step < DEG:
                    coming.append(swap(last))
            older[s], own[s], near[s] = own[s], new, coming
            if step == DEG - 1:
                every[s] = lax.all_gather(
                    jnp.concatenate(new, axis=0), "cols", axis=1, tiled=True
                ).reshape(slab_rows, -1, 1, LANES)

    whole = jnp.concatenate(every, axis=2).reshape(slab_rows, -1)
    contract = (((0,), (0,)), ((), ()))

    def products(sides):
        joined = jnp.concatenate([jnp.concatenate(side, axis=0) for side in sides], axis=1)
        terms = lax.dot_general(joined, whole, contract, preferred_element_type=jnp.float32)
        return scattered(terms.reshape(width, count // 2, 2, -1)).T / order

    return products(own), products(older)


def solution(mesh):
    in_specs = (P("rows", None), P("rows", None), P("rows"), P(), P("rows", "cols"))
    out_specs = (P("rows", "cols"), P("rows", "cols"))
    return jax.shard_map(shards, mesh=mesh, in_specs=in_specs, out_specs=out_specs, check_vma=False)
```

```python
import functools

import jax
import jax.numpy as jnp
from jax import lax
from jax.experimental import pallas as pl
from jax.experimental.pallas import tpu as pltpu
from jax.sharding import PartitionSpec as P

DEG = 4
LANES = 128
GROUP = 4
STEP = 16
PIECES = 2
WIRE = jnp.bfloat16


def mask_body(counts, ham_t, out, *, first, orbitals):
    step = first + pl.program_id(0)
    depth, lanes = ham_t.shape
    row = lax.broadcasted_iota(jnp.int32, (lanes, lanes), 0)
    col = lax.broadcasted_iota(jnp.int32, (lanes, lanes), 1)
    per = lanes // orbitals
    limit = jnp.zeros((lanes, lanes), jnp.int32)
    for i in range(per):
        limit = jnp.where(row // orbitals == i, counts[step * per + i] * orbitals, limit)
    for start in range(0, out.shape[1], lanes):
        size = min(lanes, depth - start)
        if size <= 0:
            out[:, start : start + lanes] = jnp.zeros((lanes, lanes), out.dtype)
            continue
        tile = ham_t[start : start + size, :].astype(jnp.float32)
        if size < lanes:
            tile = jnp.concatenate([tile, jnp.zeros((lanes - size, lanes), jnp.float32)], axis=0)
        tile = jnp.where(col + start < limit, tile.T, 0.0)
        out[:, start : start + lanes] = tile.astype(out.dtype)


def masked_rows(hamiltonian, counts, part, orbitals):
    depth = hamiltonian.shape[1]
    rows = hamiltonian.shape[0] // PIECES
    first = part * (rows // LANES)
    padded = pl.cdiv(depth, GROUP * orbitals) * GROUP * orbitals
    return pl.pallas_call(
        functools.partial(mask_body, first=first, orbitals=orbitals),
        out_shape=jax.ShapeDtypeStruct((rows, padded), hamiltonian.dtype),
        grid_spec=pltpu.PrefetchScalarGridSpec(
            num_scalar_prefetch=1,
            grid=(rows // LANES,),
            in_specs=[pl.BlockSpec((depth, LANES), lambda g, c: (0, first + g))],
            out_specs=pl.BlockSpec((LANES, padded), lambda g, c: (g, 0)),
        ),
        compiler_params=pltpu.CompilerParams(vmem_limit_bytes=8 << 20),
        cost_estimate=pl.CostEstimate(
            flops=rows * padded, bytes_accessed=4 * rows * padded, transcendentals=0
        ),
        name="masked_rows",
    )(counts, hamiltonian.T)


def apply_body(index, interval, *refs, kind, pieces, part, joined, orbitals):
    ham = refs[0]
    sources = refs[1 : 1 + 3 * pieces]
    at = 1 + 3 * pieces
    older = refs[at] if kind == "next" else None
    first_parts = refs[at + 1 : at + 1 + joined]
    out, extended = refs[-2 - (joined > 0)], refs[-1]
    length = sources[0].shape[0]
    tile = GROUP * orbitals
    groups = ham.shape[1] // tile
    for i, source in enumerate(sources):
        extended[i * length : (i + 1) * length, :] = source[...]
    center = (interval[0] + interval[1]) / 2.0
    half_width = (interval[1] - interval[0]) / 2.0

    def run(step, carry):
        for j in range(STEP):
            block = step * STEP + j
            rows = pl.ds(pl.multiple_of(block * orbitals, orbitals), orbitals)
            whole_rows = pl.ds(
                pl.multiple_of(part * length + block * orbitals, orbitals), orbitals
            )
            first = (part * length // orbitals + block) * groups * GROUP
            total = None
            for group in range(groups):
                parts = []
                for slot in range(group * GROUP, (group + 1) * GROUP):
                    start = pl.multiple_of(index[first + slot] * orbitals, orbitals)
                    parts.append(extended[pl.ds(start, orbitals), :])
                term = jnp.dot(
                    ham[rows, group * tile : (group + 1) * tile],
                    jnp.concatenate(parts, axis=0),
                    preferred_element_type=jnp.float32,
                )
                total = term if total is None else total + term
            if kind != "image":
                total = total - center * extended[whole_rows, :].astype(jnp.float32)
                total = total / half_width if kind == "first" else 2.0 * total / half_width
            if kind == "next":
                total = total - older[rows, :].astype(jnp.float32)
            out[rows, :] = total.astype(out.dtype)
        return carry

    lax.fori_loop(0, length // (STEP * orbitals), run, 0)
    for i, piece in enumerate((*first_parts, out) if joined else ()):
        refs[-2][i * length : (i + 1) * length, :] = piece[...]


def apply_ham(masked, index, interval, kind, part, own, near, far, older, joined, orbitals):
    pieces = len(own)
    length, width = own[0].shape
    slab = length * pieces
    padded = masked.shape[1]
    arrays = [*own, *near, *far, *([older[part]] if kind == "next" else []), *joined]
    shapes = [jax.ShapeDtypeStruct((length, width), own[0].dtype)]
    if joined:
        shapes.append(jax.ShapeDtypeStruct((slab, width), own[0].dtype))
    in_vmem = pl.BlockSpec(memory_space=pltpu.VMEM)
    return pl.pallas_call(
        functools.partial(
            apply_body, kind=kind, pieces=pieces, part=part, joined=len(joined), orbitals=orbitals
        ),
        out_shape=shapes,
        grid_spec=pltpu.PrefetchScalarGridSpec(
            num_scalar_prefetch=2,
            grid=(),
            in_specs=[in_vmem] * (1 + len(arrays)),
            out_specs=[in_vmem] * len(shapes),
            scratch_shapes=[pltpu.VMEM((3 * slab, width), own[0].dtype)],
        ),
        compiler_params=pltpu.CompilerParams(vmem_limit_bytes=8 << 20),
        cost_estimate=pl.CostEstimate(
            flops=5000000000,
            bytes_accessed=1,
            transcendentals=0,
        ),
        name="apply_" + kind,
    )(index, interval, masked, *arrays)


def after(value, *done):
    return lax.optimization_barrier((value, *done))[0]


def pair_of(i):
    return i ^ 1


def swap(piece):
    count = lax.axis_size("rows")
    return lax.ppermute(piece, "rows", [(i, pair_of(i)) for i in range(count)])


def onward(piece):
    count = lax.axis_size("rows")
    pairs = [(i, (i + 2) % count if i % 2 == 0 else (i - 2) % count) for i in range(count)]
    return lax.ppermute(piece, "rows", pairs)


def across(held, bits):
    count = lax.axis_size("cols")
    held = dict(held)
    for bit in bits:
        pairs = [(i, i ^ bit) for i in range(count)]
        for away, one in list(held.items()):
            held[away ^ bit] = lax.ppermute(one, "cols", pairs)
    return held


def product_body(column, *refs, sides, count, streams, pieces):
    out, turned = refs[-2:]
    every = refs[sides * pieces : -2]
    length, lanes = refs[0].shape
    for side in range(sides):
        for i in range(pieces):
            for start in range(0, length, lanes):
                tile = refs[side * pieces + i][start : start + lanes, :].astype(jnp.float32)
                at = i * length + start
                turned[side * lanes : (side + 1) * lanes, at : at + lanes] = tile.T.astype(
                    turned.dtype
                )
    for away in range(count):
        for s in range(streams):
            out[column[0] ^ away, s] = jnp.dot(
                turned[...], every[away * streams + s][...], preferred_element_type=jnp.float32
            )


def products(column, sides, every):
    count, streams, pieces = len(every[0]), len(every), len(sides[0])
    assert count & (count - 1) == 0
    length, lanes = sides[0][0].shape
    arrays = [piece for side in sides for piece in side]
    arrays += [every[s][away] for away in range(count) for s in range(streams)]
    in_vmem = pl.BlockSpec(memory_space=pltpu.VMEM)
    columns = len(sides) * lanes
    slab = length * pieces
    return pl.pallas_call(
        functools.partial(
            product_body, sides=len(sides), count=count, streams=streams, pieces=pieces
        ),
        out_shape=jax.ShapeDtypeStruct((count, streams, columns, lanes), jnp.float32),
        grid_spec=pltpu.PrefetchScalarGridSpec(
            num_scalar_prefetch=1,
            grid=(),
            in_specs=[in_vmem] * len(arrays),
            out_specs=in_vmem,
            scratch_shapes=[pltpu.VMEM((columns, slab), sides[0][0].dtype)],
        ),
        compiler_params=pltpu.CompilerParams(vmem_limit_bytes=8 << 20),
        cost_estimate=pl.CostEstimate(
            flops=8000000000,
            bytes_accessed=1,
            transcendentals=0,
        ),
        name="products",
    )(column[None], *arrays)


def places():
    pairs = lax.axis_size("rows") // 2
    me = lax.axis_index("rows").astype(jnp.uint32)
    half = me & 1
    around = [(me // 2 + shift) % pairs for shift in range(pairs)]
    return [lax.axis_index("cols"), half, half ^ 1, *around]


def taken(array, at, axis):
    starts = [jnp.zeros_like(at)] * array.ndim
    starts[axis] = at
    sizes = list(array.shape)
    sizes[axis] = 1
    return lax.dynamic_slice(array, starts, sizes).squeeze(axis)


def halved(terms, where):
    pairs = lax.axis_size("rows") // 2
    columns = terms.shape[2]
    terms = terms.transpose(2, 0, 1, 3).reshape(columns, pairs, 2, -1).transpose(1, 2, 0, 3)
    mine, other = taken(terms, where[1], 1), taken(terms, where[2], 1)
    return mine + swap(other.astype(WIRE)).astype(jnp.float32)


def scattered(both, where, order):
    count = lax.axis_size("rows")
    total = taken(both, where[3], 0)
    for shift in range(1, count // 2):
        hops = [(i, (i + 2 * shift) % count) for i in range(count)]
        away = lax.ppermute(taken(both, where[3 + shift], 0).astype(WIRE), "rows", hops)
        total = total + away.astype(jnp.float32)
    return total.T / order


def shards(hamiltonian, neighbors, neighbor_counts, interval, vectors):
    blocks, slots = neighbors.shape
    slab_rows = hamiltonian.shape[0]
    orbitals = slab_rows // blocks
    count = lax.axis_size("rows")
    order = slab_rows * count
    width = vectors.shape[1]
    streams = width // LANES
    length = slab_rows // PIECES

    me = lax.axis_index("rows")
    slab = neighbors // blocks
    place = jnp.where(slab == me, 0, jnp.where(slab == pair_of(me), 1, 2))
    index = place * blocks + neighbors % blocks
    padded = pl.cdiv(slots, GROUP) * GROUP
    index = jnp.concatenate(
        [index, jnp.broadcast_to(index[:, :1], (blocks, padded - slots))], axis=1
    ).reshape(-1)
    index, neighbor_counts, *where = lax.optimization_barrier(
        (index, neighbor_counts, *places())
    )

    own = [
        [
            vectors[i * length : (i + 1) * length, s * LANES : (s + 1) * LANES]
            for i in range(PIECES)
        ]
        for s in range(streams)
    ]
    older = [None] * streams
    near = [[swap(piece) for piece in own[0]]]
    masked = []
    for part in range(PIECES):
        counts = after(neighbor_counts, near[0][part - 1]) if part else neighbor_counts
        masked.append(masked_rows(hamiltonian, counts, part, orbitals))
        near[0][part] = after(near[0][part], masked[part])
    for s in range(1, streams):
        near.append([swap(after(own[s][i], masked[i])) for i in range(PIECES)])

    far = [[onward(piece) for piece in near[s]] for s in range(streams)]
    columns = lax.axis_size("cols")
    bits = [1 << i for i in range(1, columns.bit_length() - 1)]
    last = None
    held = [None] * streams
    halves = []
    for step in range(DEG + 1):
        kind = "first" if step == 0 else "next" if step < DEG else "image"
        if step == DEG:
            for s in range(streams):
                ready = {away: after(one, *near[-1]) for away, one in held[s].items()}
                held[s] = across(ready, [1])
            every = [[held[s][away] for away in range(columns)] for s in range(streams)]
        for s in range(streams):
            new, coming = [], []
            for part in range(PIECES):
                done = [] if last is None else [last]
                other = s - 1 if streams > 1 and (step > 0 or s > 0) else s
                if other != s and near[other]:
                    done.append(near[other][part])
                    done += far[other][:part]
                joined = new if step == DEG - 1 and part == PIECES - 1 else []
                last, *whole = apply_ham(
                    masked[part], after(index, *done), interval, kind, part, own[s], near[s],
                    far[s], older[s], joined, orbitals,
                )
                new.append(last)
                if step < DEG:
                    coming.append(swap(last))
            older[s], own[s], near[s] = own[s], new, coming
            far[s] = [onward(piece) for piece in coming]
            if step == DEG - 1:
                held[s] = across({0: whole[0]}, bits)
            if step == DEG:
                sides = [new] + ([older[0]] + own[1:] if s == 0 else [])
                last = products(after(where[0], *halves), sides, every)
                halves.append(halved(last, where))
    sums = [scattered(both, where, order) for both in halves]
    projected = jnp.concatenate([sums[0][:, :LANES]] + sums[1:], axis=1)
    return projected, sums[0][:, LANES:]


def solution(mesh):
    in_specs = (P("rows", None), P("rows", None), P("rows"), P(), P("rows", "cols"))
    out_specs = (P("rows", "cols"), P("rows", "cols"))
    return jax.shard_map(shards, mesh=mesh, in_specs=in_specs, out_specs=out_specs, check_vma=False)
```

```python
import functools

import jax
import jax.numpy as jnp
from jax import lax
from jax.experimental import pallas as pl
from jax.experimental.pallas import tpu as pltpu
from jax.sharding import PartitionSpec as P

DEG = 4
LANES = 128
GROUP = 4
STEP = 16
PIECES = 2
WIRE = jnp.bfloat16


def mask_body(counts, ham_t, out, *, first, orbitals):
    step = first + pl.program_id(0)
    depth, lanes = ham_t.shape
    row = lax.broadcasted_iota(jnp.int32, (lanes, lanes), 0)
    col = lax.broadcasted_iota(jnp.int32, (lanes, lanes), 1)
    per = lanes // orbitals
    limit = jnp.zeros((lanes, lanes), jnp.int32)
    for i in range(per):
        limit = jnp.where(row // orbitals == i, counts[step * per + i] * orbitals, limit)
    for start in range(0, out.shape[1], lanes):
        size = min(lanes, depth - start)
        if size <= 0:
            out[:, start : start + lanes] = jnp.zeros((lanes, lanes), out.dtype)
            continue
        tile = ham_t[start : start + size, :].astype(jnp.float32)
        if size < lanes:
            tile = jnp.concatenate([tile, jnp.zeros((lanes - size, lanes), jnp.float32)], axis=0)
        tile = jnp.where(col + start < limit, tile.T, 0.0)
        out[:, start : start + lanes] = tile.astype(out.dtype)


def masked_rows(hamiltonian, counts, part, orbitals):
    depth = hamiltonian.shape[1]
    rows = hamiltonian.shape[0] // PIECES
    first = part * (rows // LANES)
    padded = pl.cdiv(depth, GROUP * orbitals) * GROUP * orbitals
    return pl.pallas_call(
        functools.partial(mask_body, first=first, orbitals=orbitals),
        out_shape=jax.ShapeDtypeStruct((rows, padded), hamiltonian.dtype),
        grid_spec=pltpu.PrefetchScalarGridSpec(
            num_scalar_prefetch=1,
            grid=(rows // LANES,),
            in_specs=[pl.BlockSpec((depth, LANES), lambda g, c: (0, first + g))],
            out_specs=pl.BlockSpec((LANES, padded), lambda g, c: (g, 0)),
        ),
        compiler_params=pltpu.CompilerParams(vmem_limit_bytes=8 << 20),
        cost_estimate=pl.CostEstimate(
            flops=rows * padded, bytes_accessed=4 * rows * padded, transcendentals=0
        ),
        name="masked_rows",
    )(counts, hamiltonian.T)


def apply_body(index, interval, *refs, kind, pieces, part, joined, orbitals):
    ham = refs[0]
    sources = refs[1 : 1 + 3 * pieces]
    at = 1 + 3 * pieces
    older = refs[at] if kind == "next" else None
    first_parts = refs[at + 1 : at + 1 + joined]
    out, extended = refs[-2 - (joined > 0)], refs[-1]
    length = sources[0].shape[0]
    tile = GROUP * orbitals
    groups = ham.shape[1] // tile
    for i, source in enumerate(sources):
        extended[i * length : (i + 1) * length, :] = source[...]
    center = (interval[0] + interval[1]) / 2.0
    half_width = (interval[1] - interval[0]) / 2.0

    def run(step, carry):
        for j in range(STEP):
            block = step * STEP + j
            rows = pl.ds(pl.multiple_of(block * orbitals, orbitals), orbitals)
            whole_rows = pl.ds(
                pl.multiple_of(part * length + block * orbitals, orbitals), orbitals
            )
            first = (part * length // orbitals + block) * groups * GROUP
            total = None
            for group in range(groups):
                parts = []
                for slot in range(group * GROUP, (group + 1) * GROUP):
                    start = pl.multiple_of(index[first + slot] * orbitals, orbitals)
                    parts.append(extended[pl.ds(start, orbitals), :])
                term = jnp.dot(
                    ham[rows, group * tile : (group + 1) * tile],
                    jnp.concatenate(parts, axis=0),
                    preferred_element_type=jnp.float32,
                )
                total = term if total is None else total + term
            if kind != "image":
                total = total - center * extended[whole_rows, :].astype(jnp.float32)
                total = total / half_width if kind == "first" else 2.0 * total / half_width
            if kind == "next":
                total = total - older[rows, :].astype(jnp.float32)
            out[rows, :] = total.astype(out.dtype)
        return carry

    lax.fori_loop(0, length // (STEP * orbitals), run, 0)
    for i, piece in enumerate((*first_parts, out) if joined else ()):
        refs[-2][i * length : (i + 1) * length, :] = piece[...]


def apply_ham(masked, index, interval, kind, part, own, near, far, older, joined, orbitals):
    pieces = len(own)
    length, width = own[0].shape
    slab = length * pieces
    padded = masked.shape[1]
    arrays = [*own, *near, *far, *([older[part]] if kind == "next" else []), *joined]
    shapes = [jax.ShapeDtypeStruct((length, width), own[0].dtype)]
    if joined:
        shapes.append(jax.ShapeDtypeStruct((slab, width), own[0].dtype))
    in_vmem = pl.BlockSpec(memory_space=pltpu.VMEM)
    return pl.pallas_call(
        functools.partial(
            apply_body, kind=kind, pieces=pieces, part=part, joined=len(joined), orbitals=orbitals
        ),
        out_shape=shapes,
        grid_spec=pltpu.PrefetchScalarGridSpec(
            num_scalar_prefetch=2,
            grid=(),
            in_specs=[in_vmem] * (1 + len(arrays)),
            out_specs=[in_vmem] * len(shapes),
            scratch_shapes=[pltpu.VMEM((3 * slab, width), own[0].dtype)],
        ),
        compiler_params=pltpu.CompilerParams(vmem_limit_bytes=8 << 20),
        cost_estimate=pl.CostEstimate(
            flops=5_000_000_000,
            bytes_accessed=1,
            transcendentals=0,
        ),
        name="apply_" + kind,
    )(index, interval, masked, *arrays)


def after(value, *done):
    return lax.optimization_barrier((value, *done))[0]


def pair_of(i):
    return i ^ 1


def swap(piece):
    count = lax.axis_size("rows")
    return lax.ppermute(piece, "rows", [(i, pair_of(i)) for i in range(count)])


def onward(piece):
    count = lax.axis_size("rows")
    pairs = [(i, (i + 2) % count if i % 2 == 0 else (i - 2) % count) for i in range(count)]
    return lax.ppermute(piece, "rows", pairs)


def across(held, bits):
    count = lax.axis_size("cols")
    held = dict(held)
    for bit in bits:
        pairs = [(i, i ^ bit) for i in range(count)]
        for away, one in list(held.items()):
            held[away ^ bit] = lax.ppermute(one, "cols", pairs)
    return held


def product_body(column, *refs, sides, count, streams, pieces):
    out, turned = refs[-2:]
    every = refs[sides * pieces : -2]
    length, lanes = refs[0].shape
    for side in range(sides):
        for i in range(pieces):
            for start in range(0, length, lanes):
                tile = refs[side * pieces + i][start : start + lanes, :].astype(jnp.float32)
                at = i * length + start
                turned[side * lanes : (side + 1) * lanes, at : at + lanes] = tile.T.astype(
                    turned.dtype
                )
    for away in range(count):
        for s in range(streams):
            out[column[0] ^ away, s] = jnp.dot(
                turned[...], every[away * streams + s][...], preferred_element_type=jnp.float32
            ).T


def products(column, sides, every):
    count, streams, pieces = len(every[0]), len(every), len(sides[0])
    assert count & (count - 1) == 0
    length, lanes = sides[0][0].shape
    arrays = [piece for side in sides for piece in side]
    arrays += [every[s][away] for away in range(count) for s in range(streams)]
    in_vmem = pl.BlockSpec(memory_space=pltpu.VMEM)
    columns = len(sides) * lanes
    slab = length * pieces
    return pl.pallas_call(
        functools.partial(
            product_body, sides=len(sides), count=count, streams=streams, pieces=pieces
        ),
        out_shape=jax.ShapeDtypeStruct((count, streams, lanes, columns), jnp.float32),
        grid_spec=pltpu.PrefetchScalarGridSpec(
            num_scalar_prefetch=1,
            grid=(),
            in_specs=[in_vmem] * len(arrays),
            out_specs=in_vmem,
            scratch_shapes=[pltpu.VMEM((columns, slab), sides[0][0].dtype)],
        ),
        compiler_params=pltpu.CompilerParams(vmem_limit_bytes=8 << 20),
        cost_estimate=pl.CostEstimate(
            flops=1,
            bytes_accessed=1,
            transcendentals=0,
        ),
        name="products",
    )(column[None], *arrays)


def places():
    pairs = lax.axis_size("rows") // 2
    me = lax.axis_index("rows").astype(jnp.uint32)
    half = me & 1
    around = [(me // 2 + shift) % pairs for shift in range(pairs)]
    return [lax.axis_index("cols"), half, half ^ 1, *around]


def taken(array, at, axis):
    starts = [jnp.zeros_like(at)] * array.ndim
    starts[axis] = at
    sizes = list(array.shape)
    sizes[axis] = 1
    return lax.dynamic_slice(array, starts, sizes).squeeze(axis)


def halved(terms, where):
    pairs = lax.axis_size("rows") // 2
    terms = terms.reshape(pairs, 2, -1, terms.shape[3])
    mine, other = taken(terms, where[1], 1), taken(terms, where[2], 1)
    return mine + swap(other.astype(WIRE)).astype(jnp.float32)


def scattered(both, where, order):
    count = lax.axis_size("rows")
    total = taken(both, where[3], 0)
    for shift in range(1, count // 2):
        hops = [(i, (i + 2 * shift) % count) for i in range(count)]
        away = lax.ppermute(taken(both, where[3 + shift], 0).astype(WIRE), "rows", hops)
        total = total + away.astype(jnp.float32)
    return total / order


def shards(hamiltonian, neighbors, neighbor_counts, interval, vectors):
    blocks, slots = neighbors.shape
    slab_rows = hamiltonian.shape[0]
    orbitals = slab_rows // blocks
    count = lax.axis_size("rows")
    order = slab_rows * count
    width = vectors.shape[1]
    streams = width // LANES
    length = slab_rows // PIECES

    me = lax.axis_index("rows")
    slab = neighbors // blocks
    place = jnp.where(slab == me, 0, jnp.where(slab == pair_of(me), 1, 2))
    index = place * blocks + neighbors % blocks
    padded = pl.cdiv(slots, GROUP) * GROUP
    index = jnp.concatenate(
        [index, jnp.broadcast_to(index[:, :1], (blocks, padded - slots))], axis=1
    ).reshape(-1)
    index, neighbor_counts, *where = lax.optimization_barrier(
        (index, neighbor_counts, *places())
    )

    own = [
        [
            vectors[i * length : (i + 1) * length, s * LANES : (s + 1) * LANES]
            for i in range(PIECES)
        ]
        for s in range(streams)
    ]
    older = [None] * streams
    near = [[swap(piece) for piece in own[0]]]
    masked = []
    for part in range(PIECES):
        counts = after(neighbor_counts, near[0][part - 1]) if part else neighbor_counts
        masked.append(masked_rows(hamiltonian, counts, part, orbitals))
        near[0][part] = after(near[0][part], masked[part])
    for s in range(1, streams):
        near.append([swap(after(own[s][i], masked[i])) for i in range(PIECES)])

    far = [[onward(piece) for piece in near[s]] for s in range(streams)]
    columns = lax.axis_size("cols")
    bits = [1 << i for i in range(1, columns.bit_length() - 1)]
    last = None
    held = [None] * streams
    halves = []
    for step in range(DEG + 1):
        kind = "first" if step == 0 else "next" if step < DEG else "image"
        for s in range(streams):
            new, coming = [], []
            for part in range(PIECES):
                done = [] if last is None else [last]
                other = s - 1 if streams > 1 and (step > 0 or s > 0) else s
                if other != s and near[other]:
                    done.append(near[other][part])
                    done += far[other][:part]
                joined = new if step == DEG - 1 and part == PIECES - 1 else []
                last, *whole = apply_ham(
                    masked[part], after(index, *done), interval, kind, part, own[s], near[s],
                    far[s], older[s], joined, orbitals,
                )
                new.append(last)
                if step == DEG and s == 0 and part == 0:
                    for t in range(streams):
                        ready = {away: after(one, last) for away, one in held[t].items()}
                        held[t] = across(ready, [1])
                if step < DEG:
                    coming.append(swap(last))
            older[s], own[s], near[s] = own[s], new, coming
            far[s] = [onward(piece) for piece in coming]
            if step == DEG - 1:
                held[s] = across({0: whole[0]}, bits)
            if step == DEG:
                every = [[h[away] for away in range(columns)] for h in held]
                sides = [new] + ([older[0]] + own[1:] if s == 0 else [])
                last = products(after(where[0], *halves), sides, every)
                halves.append(halved(last, where))
    sums = [scattered(both, where, order) for both in halves]
    projected = jnp.concatenate([sums[0][:, :LANES]] + sums[1:], axis=1)
    return projected, sums[0][:, LANES:]


def solution(mesh):
    in_specs = (P("rows", None), P("rows", None), P("rows"), P(), P("rows", "cols"))
    out_specs = (P("rows", "cols"), P("rows", "cols"))
    return jax.shard_map(shards, mesh=mesh, in_specs=in_specs, out_specs=out_specs, check_vma=False)
```

```python
import functools

import jax
import jax.numpy as jnp
from jax import lax
from jax.experimental import pallas as pl
from jax.experimental.pallas import tpu as pltpu
from jax.sharding import PartitionSpec as P

DEG = 4
LANES = 128
GROUP = 4
STEP = 16
PIECES = 2
WIRE = jnp.bfloat16


def mask_body(counts, ham_t, out, *, first, orbitals):
    step = first + pl.program_id(0)
    depth, lanes = ham_t.shape
    row = lax.broadcasted_iota(jnp.int32, (lanes, lanes), 0)
    col = lax.broadcasted_iota(jnp.int32, (lanes, lanes), 1)
    per = lanes // orbitals
    limit = jnp.zeros((lanes, lanes), jnp.int32)
    for i in range(per):
        limit = jnp.where(row // orbitals == i, counts[step * per + i] * orbitals, limit)
    for start in range(0, out.shape[1], lanes):
        size = min(lanes, depth - start)
        if size <= 0:
            out[:, start : start + lanes] = jnp.zeros((lanes, lanes), out.dtype)
            continue
        tile = ham_t[start : start + size, :].astype(jnp.float32)
        if size < lanes:
            tile = jnp.concatenate([tile, jnp.zeros((lanes - size, lanes), jnp.float32)], axis=0)
        tile = jnp.where(col + start < limit, tile.T, 0.0)
        out[:, start : start + lanes] = tile.astype(out.dtype)


def masked_rows(hamiltonian, counts, part, orbitals):
    depth = hamiltonian.shape[1]
    rows = hamiltonian.shape[0] // PIECES
    first = part * (rows // LANES)
    padded = pl.cdiv(depth, GROUP * orbitals) * GROUP * orbitals
    return pl.pallas_call(
        functools.partial(mask_body, first=first, orbitals=orbitals),
        out_shape=jax.ShapeDtypeStruct((rows, padded), hamiltonian.dtype),
        grid_spec=pltpu.PrefetchScalarGridSpec(
            num_scalar_prefetch=1,
            grid=(rows // LANES,),
            in_specs=[pl.BlockSpec((depth, LANES), lambda g, c: (0, first + g))],
            out_specs=pl.BlockSpec((LANES, padded), lambda g, c: (g, 0)),
        ),
        compiler_params=pltpu.CompilerParams(vmem_limit_bytes=8 << 20),
        cost_estimate=pl.CostEstimate(
            flops=rows * padded, bytes_accessed=4 * rows * padded, transcendentals=0
        ),
        name="masked_rows",
    )(counts, hamiltonian.T)


def apply_body(index, interval, *refs, kind, pieces, part, joined, orbitals):
    ham = refs[0]
    sources = refs[1 : 1 + 3 * pieces]
    at = 1 + 3 * pieces
    older = refs[at] if kind == "next" else None
    first_parts = refs[at + 1 : at + 1 + joined]
    out, extended = refs[-2 - (joined > 0)], refs[-1]
    length = sources[0].shape[0]
    tile = GROUP * orbitals
    groups = ham.shape[1] // tile
    for i, source in enumerate(sources):
        extended[i * length : (i + 1) * length, :] = source[...]
    center = (interval[0] + interval[1]) / 2.0
    half_width = (interval[1] - interval[0]) / 2.0

    def run(step, carry):
        for j in range(STEP):
            block = step * STEP + j
            rows = pl.ds(pl.multiple_of(block * orbitals, orbitals), orbitals)
            whole_rows = pl.ds(
                pl.multiple_of(part * length + block * orbitals, orbitals), orbitals
            )
            first = (part * length // orbitals + block) * groups * GROUP
            total = None
            for group in range(groups):
                parts = []
                for slot in range(group * GROUP, (group + 1) * GROUP):
                    start = pl.multiple_of(index[first + slot] * orbitals, orbitals)
                    parts.append(extended[pl.ds(start, orbitals), :])
                term = jnp.dot(
                    ham[rows, group * tile : (group + 1) * tile],
                    jnp.concatenate(parts, axis=0),
                    preferred_element_type=jnp.float32,
                )
                total = term if total is None else total + term
            if kind != "image":
                total = total - center * extended[whole_rows, :].astype(jnp.float32)
                total = total / half_width if kind == "first" else 2.0 * total / half_width
            if kind == "next":
                total = total - older[rows, :].astype(jnp.float32)
            out[rows, :] = total.astype(out.dtype)
        return carry

    lax.fori_loop(0, length // (STEP * orbitals), run, 0)
    for i, piece in enumerate((*first_parts, out) if joined else ()):
        refs[-2][i * length : (i + 1) * length, :] = piece[...]


def apply_ham(masked, index, interval, kind, part, own, near, far, older, joined, orbitals):
    pieces = len(own)
    length, width = own[0].shape
    slab = length * pieces
    padded = masked.shape[1]
    arrays = [*own, *near, *far, *([older[part]] if kind == "next" else []), *joined]
    shapes = [jax.ShapeDtypeStruct((length, width), own[0].dtype)]
    if joined:
        shapes.append(jax.ShapeDtypeStruct((slab, width), own[0].dtype))
    in_vmem = pl.BlockSpec(memory_space=pltpu.VMEM)
    return pl.pallas_call(
        functools.partial(
            apply_body, kind=kind, pieces=pieces, part=part, joined=len(joined), orbitals=orbitals
        ),
        out_shape=shapes,
        grid_spec=pltpu.PrefetchScalarGridSpec(
            num_scalar_prefetch=2,
            grid=(),
            in_specs=[in_vmem] * (1 + len(arrays)),
            out_specs=[in_vmem] * len(shapes),
            scratch_shapes=[pltpu.VMEM((3 * slab, width), own[0].dtype)],
        ),
        compiler_params=pltpu.CompilerParams(vmem_limit_bytes=8 << 20),
        cost_estimate=pl.CostEstimate(
            flops=5_000_000_000 if kind == "image" else 1_000_000_000,
            bytes_accessed=1,
            transcendentals=0,
        ),
        name="apply_" + kind,
    )(index, interval, masked, *arrays)


def after(value, *done):
    return lax.optimization_barrier((value, *done))[0]


def pair_of(i):
    return i ^ 1


def swap(piece):
    count = lax.axis_size("rows")
    return lax.ppermute(piece, "rows", [(i, pair_of(i)) for i in range(count)])


def onward(piece):
    count = lax.axis_size("rows")
    pairs = [(i, (i + 2) % count if i % 2 == 0 else (i - 2) % count) for i in range(count)]
    return lax.ppermute(piece, "rows", pairs)


def across(held, bits):
    count = lax.axis_size("cols")
    held = dict(held)
    for bit in bits:
        pairs = [(i, i ^ bit) for i in range(count)]
        for away, one in list(held.items()):
            held[away ^ bit] = lax.ppermute(one, "cols", pairs)
    return held


def product_body(column, *refs, sides, count, streams, pieces):
    out, turned = refs[-2:]
    every = refs[sides * pieces : -2]
    length, lanes = refs[0].shape
    for side in range(sides):
        for i in range(pieces):
            for start in range(0, length, lanes):
                tile = refs[side * pieces + i][start : start + lanes, :].astype(jnp.float32)
                at = i * length + start
                turned[side * lanes : (side + 1) * lanes, at : at + lanes] = tile.T.astype(
                    turned.dtype
                )
    for away in range(count):
        for s in range(streams):
            out[column[0] ^ away, s] = jnp.dot(
                turned[...], every[away * streams + s][...], preferred_element_type=jnp.float32
            ).T


def products(column, sides, every):
    count, streams, pieces = len(every[0]), len(every), len(sides[0])
    assert count & (count - 1) == 0
    length, lanes = sides[0][0].shape
    arrays = [piece for side in sides for piece in side]
    arrays += [every[s][away] for away in range(count) for s in range(streams)]
    in_vmem = pl.BlockSpec(memory_space=pltpu.VMEM)
    columns = len(sides) * lanes
    slab = length * pieces
    return pl.pallas_call(
        functools.partial(
            product_body, sides=len(sides), count=count, streams=streams, pieces=pieces
        ),
        out_shape=jax.ShapeDtypeStruct((count, streams, lanes, columns), jnp.float32),
        grid_spec=pltpu.PrefetchScalarGridSpec(
            num_scalar_prefetch=1,
            grid=(),
            in_specs=[in_vmem] * len(arrays),
            out_specs=in_vmem,
            scratch_shapes=[pltpu.VMEM((columns, slab), sides[0][0].dtype)],
        ),
        compiler_params=pltpu.CompilerParams(vmem_limit_bytes=8 << 20),
        cost_estimate=pl.CostEstimate(
            flops=1,
            bytes_accessed=1,
            transcendentals=0,
        ),
        name="products",
    )(column[None], *arrays)


def places():
    pairs = lax.axis_size("rows") // 2
    me = lax.axis_index("rows").astype(jnp.uint32)
    half = me & 1
    around = [(me // 2 + shift) % pairs for shift in range(pairs)]
    return [lax.axis_index("cols"), half, half ^ 1, *around]


def taken(array, at, axis):
    starts = [jnp.zeros_like(at)] * array.ndim
    starts[axis] = at
    sizes = list(array.shape)
    sizes[axis] = 1
    return lax.dynamic_slice(array, starts, sizes).squeeze(axis)


def halved(terms, where):
    pairs = lax.axis_size("rows") // 2
    terms = terms.reshape(pairs, 2, -1, terms.shape[3])
    mine, other = taken(terms, where[1], 1), taken(terms, where[2], 1)
    return mine + swap(other.astype(WIRE)).astype(jnp.float32)


def scattered(both, where, order):
    count = lax.axis_size("rows")
    total = taken(both, where[3], 0)
    for shift in range(1, count // 2):
        hops = [(i, (i + 2 * shift) % count) for i in range(count)]
        away = lax.ppermute(taken(both, where[3 + shift], 0).astype(WIRE), "rows", hops)
        total = total + away.astype(jnp.float32)
    return total / order


def shards(hamiltonian, neighbors, neighbor_counts, interval, vectors):
    blocks, slots = neighbors.shape
    slab_rows = hamiltonian.shape[0]
    orbitals = slab_rows // blocks
    count = lax.axis_size("rows")
    order = slab_rows * count
    width = vectors.shape[1]
    streams = width // LANES
    length = slab_rows // PIECES

    me = lax.axis_index("rows")
    slab = neighbors // blocks
    place = jnp.where(slab == me, 0, jnp.where(slab == pair_of(me), 1, 2))
    index = place * blocks + neighbors % blocks
    padded = pl.cdiv(slots, GROUP) * GROUP
    index = jnp.concatenate(
        [index, jnp.broadcast_to(index[:, :1], (blocks, padded - slots))], axis=1
    ).reshape(-1)
    index, neighbor_counts, *where = lax.optimization_barrier(
        (index, neighbor_counts, *places())
    )

    own = [
        [
            vectors[i * length : (i + 1) * length, s * LANES : (s + 1) * LANES]
            for i in range(PIECES)
        ]
        for s in range(streams)
    ]
    older = [None] * streams
    near = [[swap(piece) for piece in own[0]]]
    masked = []
    for part in range(PIECES):
        counts = after(neighbor_counts, near[0][part - 1]) if part else neighbor_counts
        masked.append(masked_rows(hamiltonian, counts, part, orbitals))
        near[0][part] = after(near[0][part], masked[part])
    for s in range(1, streams):
        near.append([swap(after(own[s][i], masked[i])) for i in range(PIECES)])

    far = [[onward(piece) for piece in near[s]] for s in range(streams)]
    columns = lax.axis_size("cols")
    bits = [1 << i for i in range(1, columns.bit_length() - 1)]
    last = None
    held = [None] * streams
    halves = []
    for step in range(DEG + 1):
        kind = "first" if step == 0 else "next" if step < DEG else "image"
        for s in range(streams):
            new, coming = [], []
            for part in range(PIECES):
                done = [] if last is None else [last]
                other = s - 1 if streams > 1 and (step > 0 or s > 0) else s
                if other != s and near[other]:
                    done.append(near[other][part])
                    done += far[other][:part]
                joined = new if step == DEG - 1 and part == PIECES - 1 else []
                last, *whole = apply_ham(
                    masked[part], after(index, *done), interval, kind, part, own[s], near[s],
                    far[s], older[s], joined, orbitals,
                )
                new.append(last)
                if step == DEG and s == 0 and part == 0:
                    for t in range(streams):
                        ready = {away: after(one, last) for away, one in held[t].items()}
                        held[t] = across(ready, [1])
                if step < DEG:
                    coming.append(swap(last))
            older[s], own[s], near[s] = own[s], new, coming
            far[s] = [onward(piece) for piece in coming]
            if step == DEG - 1:
                held[s] = across({0: whole[0]}, bits)
            if step == DEG:
                every = [[h[away] for away in range(columns)] for h in held]
                sides = [new] + ([older[0]] + own[1:] if s == 0 else [])
                last = products(after(where[0], *halves), sides, every)
                halves.append(halved(last, where))
    sums = [scattered(both, where, order) for both in halves]
    projected = jnp.concatenate([sums[0][:, :LANES]] + sums[1:], axis=1)
    return projected, sums[0][:, LANES:]


def solution(mesh):
    in_specs = (P("rows", None), P("rows", None), P("rows"), P(), P("rows", "cols"))
    out_specs = (P("rows", "cols"), P("rows", "cols"))
    return jax.shard_map(shards, mesh=mesh, in_specs=in_specs, out_specs=out_specs, check_vma=False)
```
